128 devices in a mesh: leaf: 16 (over x, y_lo, core), panel: 8 (over z, y_hi).
Axes of the slice: x: 4, y: 4 (y_hi: 2, y_lo: 2; y = y_hi * 2 + y_lo), z: 4, core: 2. Of those that a mesh axis runs over, the one named last changes fastest.
Arguments:
- ext_rows: bfloat16 [16, 4608, 5120], P('leaf', 'panel'), as said below
- iface_rows: bfloat16 [16, 512, 5120], P('leaf', 'panel'), as said below
- inverse: bfloat16 [16, 512, 512], P('leaf', 'panel'), as said below
- pivot: int32 [16, 256], P('leaf'), may hold values from 0 to 255, as said below
- flags: int32 [16, 9], P('leaf'), may hold values 0 or 1
Outputs:
- merged: bfloat16 [16, 4608, 9216], P('leaf', 'panel')
The draws below stay inside these ranges and needn't reach their ends.
Inputs may be any that keep to these rules, and one draw needn't show every extreme that they name: `pivot`: each row is a permutation of 0 to 255; the rows of two merge partners are inverse to each other. `ext_rows`: each 2 x 2 block of real entries is the real form [[a, -b], [b, a]] of one complex number. `iface_rows`: each 2 x 2 block of real entries is the real form [[a, -b], [b, a]] of one complex number. `inverse`: each 2 x 2 block of real entries is the real form [[a, -b], [b, a]] of one complex number.
All inputs are finite; a program needn't handle non-finite values. No bound on the sum of `flags` on one device may be relied on, other than what follows from the above.
Results may differ from the reference program's by a relative error of at most 0.005.
Values may be sent and summed in bfloat16 or wider, within the bound.
No kernel may reach another device: no remote copies, remote signals or barrier semaphores. Data moves between devices by JAX's collectives and lax.ppermute only.
A program may use at most 128 MiB of HBM per device.

```python
import jax
import jax.numpy as jnp
from jax import lax

EFACES = 9
BIT = 2
IPTS = 256
IDIM = 512
EDIM = 4608
LEAVES = 16


def complex_blocks(key, rows, cols, scale):
    first, second = jax.random.split(key)
    real_part = jax.random.normal(first, (rows, cols), jnp.float32) * scale
    imag_part = jax.random.normal(second, (rows, cols), jnp.float32) * scale
    upper = jnp.stack([real_part, -imag_part], axis=-1)
    lower = jnp.stack([imag_part, real_part], axis=-1)
    return jnp.stack([upper, lower], axis=1).reshape(2 * rows, 2 * cols)


def draw_ext_rows(key, part):
    first, second = jax.random.split(jax.random.fold_in(key, 11))
    direct = complex_blocks(first, LEAVES * EDIM // 2, EDIM // 2, 1.0).reshape(LEAVES, EDIM, EDIM)
    across = complex_blocks(second, LEAVES * EDIM // 2, IDIM // 2, IDIM ** (-0.5)).reshape(LEAVES, EDIM, IDIM)
    return jnp.concatenate([direct, across], axis=2).astype(jnp.bfloat16)


def draw_iface_rows(key, part):
    first, second = jax.random.split(jax.random.fold_in(key, 23))
    outward = complex_blocks(first, LEAVES * IDIM // 2, EDIM // 2, 1.0).reshape(LEAVES, IDIM, EDIM)
    inward = complex_blocks(second, LEAVES * IDIM // 2, IDIM // 2, IDIM ** (-0.5)).reshape(LEAVES, IDIM, IDIM)
    return jnp.concatenate([outward, inward], axis=2).astype(jnp.bfloat16)


def draw_inverse(key, part):
    noise = complex_blocks(jax.random.fold_in(key, 37), LEAVES * IDIM // 2, IDIM // 2, 0.5 * IDIM ** (-0.5))
    eye = jnp.eye(IDIM, dtype=jnp.float32)[None, :, :]
    return (eye + noise.reshape(LEAVES, IDIM, IDIM)).astype(jnp.bfloat16)


def draw_pivot(key, part):
    pair_keys = jax.random.split(jax.random.fold_in(key, 51), LEAVES // 2)
    perms = jax.vmap(lambda one: jax.random.permutation(one, IPTS))(pair_keys).astype(jnp.int32)
    inverse_perms = jnp.argsort(perms, axis=1).astype(jnp.int32)
    leaves = jnp.arange(LEAVES, dtype=jnp.int32)
    low = leaves % 2 ** BIT
    pair = leaves // 2 ** (BIT + 1) * 2 ** BIT + low
    side = leaves // 2 ** BIT % 2
    return jnp.where(side[:, None] == 0, perms[pair], inverse_perms[pair]).astype(jnp.int32)


def plant(array, own_key, least, largest):
    shape = array.shape
    index_at = [jax.random.randint(jax.random.fold_in(own_key, axis), (), 0, shape[axis]) for axis in range(len(shape))]
    array = array.at[tuple(index_at)].set(least)
    longest = shape.index(max(shape))
    index_at[longest] = (index_at[longest] + 1) % shape[longest]
    return array.at[tuple(index_at)].set(largest)


def setup_inputs(seed: int = 0) -> dict:
    key_of = jax.random.split(jax.random.key(seed), 6)
    ext_rows = draw_ext_rows(jax.random.fold_in(key_of[5], 71), 0)
    iface_rows = draw_iface_rows(jax.random.fold_in(key_of[5], 71), 0)
    inverse = draw_inverse(jax.random.fold_in(key_of[5], 71), 0)
    pivot = draw_pivot(jax.random.fold_in(key_of[5], 71), 0)
    flags = plant((jax.random.randint(key_of[4], (LEAVES, EFACES), 0, 2) < 1).astype(jnp.int32), jax.random.fold_in(key_of[4], 1), 0, 1)
    return dict(ext_rows=ext_rows, iface_rows=iface_rows, inverse=inverse, pivot=pivot, flags=flags)


def merge_one(items):
    ext, iface, iface_partner, winv, piv, flag = items
    idim = winv.shape[1]
    edim = ext.shape[1] - idim
    direct_block = ext[:, :edim].astype(jnp.float32)
    ext_to_iface = ext[:, edim:]
    own_rows = iface[:, :edim]
    partner_rows = iface_partner[:, :edim]
    partner_block = iface_partner[:, edim:]
    order = (2 * piv[:, None] + jnp.arange(2, dtype=jnp.int32)[None, :]).reshape(-1).astype(jnp.int32)
    back = jnp.argsort(order).astype(jnp.int32)
    permuted = jnp.take(winv, back, axis=1)
    coupled = jnp.dot(ext_to_iface, permuted, preferred_element_type=jnp.float32).astype(jnp.bfloat16)
    through = jnp.dot(coupled, jnp.take(partner_block, order, axis=1), preferred_element_type=jnp.float32).astype(jnp.bfloat16)
    own = direct_block + jnp.dot(through, own_rows, preferred_element_type=jnp.float32)
    cross = jnp.dot(coupled, partner_rows, preferred_element_type=jnp.float32).astype(jnp.bfloat16)
    sign = 1.0 - 2.0 * jnp.repeat(flag, edim // flag.shape[0]).astype(jnp.float32)
    whole = jnp.concatenate([own, cross.astype(jnp.float32)], axis=1)
    return (sign[:, None] * whole).astype(jnp.bfloat16)


def reference(ext_rows, iface_rows, inverse, pivot, flags):
    leaves = jnp.arange(LEAVES, dtype=jnp.int32)
    partner = jnp.bitwise_xor(leaves, jnp.int32(2 ** BIT))
    iface_partner = jnp.take(iface_rows, partner, axis=0)
    return lax.map(merge_one, (ext_rows, iface_rows, iface_partner, inverse, pivot, flags))
```

```python
import functools

import jax
import jax.numpy as jnp
from jax import lax
from jax.experimental import pallas as pl
from jax.experimental.pallas import tpu as pltpu
from jax.sharding import PartitionSpec as P


FPTS = 256
BIT = 2
TILE = 512
F32 = jnp.float32
BF16 = jnp.bfloat16


def iota(shape, axis):
    return lax.broadcasted_iota(jnp.int32, shape, axis)


def dot(a, b):
    return jnp.dot(a, b, preferred_element_type=F32)


def row_sign(flags_ref, rows):
    first = lax.axis_index("panel") * rows
    face = (first + iota((rows, 1), 0)) // (2 * FPTS)
    sign = jnp.ones((rows, 1), F32)
    for f in range(flags_ref.shape[1]):
        sign = jnp.where((face == f) & (flags_ref[0, f] == 1), -1.0, sign)
    return sign


def split_kernel(iface_ref, winv_ref, first_ref, own_ref, far_ref):
    rows = iface_ref.shape[0]
    half = rows // 2
    c0 = first_ref.shape[1]
    idim = winv_ref.shape[1]
    edim = iface_ref.shape[1] - idim
    pick = (iota((half, rows), 1) == 2 * iota((half, rows), 0)).astype(BF16)
    even = dot(pick, iface_ref[...]).astype(BF16)
    winv = dot(pick, winv_ref[...]).astype(BF16)
    col = iota((idim, idim), 1)
    src = jnp.where(col < idim // 2, 2 * col, 2 * col - idim + 1)
    deint = (iota((idim, idim), 0) == src).astype(BF16)
    first_ref[...] = even[:, :c0]
    own_ref[:, idim:] = even[:, c0:edim]
    far_ref[:, idim:] = even[:, c0:edim]
    own_ref[:, :idim] = dot(winv, deint).astype(BF16)
    far_ref[:, :idim] = dot(even[:, edim:], deint).astype(BF16)


def place(pieces, refs, dst, cols):
    panel = lax.axis_index("panel")
    z, y = panel // 2, panel % 2
    for which, offset, dz, dy in pieces:
        where = ((z + 4 + dz) % 4) * 2 + (y + dy) % 2
        n = 32
        dst[pl.ds(pl.multiple_of(where * n, n), n), :] = refs[which][offset : offset + n, cols]


def couple_kernel(own_pieces, far_pieces, n_in, ext_ref, pivot_ref, flags_ref, *rest):
    refs = rest[:n_in]
    coupled_ref, through_ref, w_ref, q_ref = rest[n_in:]
    rows = ext_ref.shape[0]
    idim = ext_ref.shape[1]
    half = idim // 2
    place(own_pieces, refs, w_ref, slice(0, idim))
    place(far_pieces, refs, q_ref, slice(0, idim))
    col = iota((idim, idim), 1)
    src = jnp.where(col < half, 2 * col, 2 * col - idim + 1)
    deint = (iota((idim, idim), 0) == src).astype(BF16)
    across = dot(ext_ref[...], deint).astype(BF16)
    onehot = (iota((half, half), 0) == pivot_ref[...]).astype(BF16)

    def times(lhs, even_ref):
        a, nb = even_ref[:, :half], even_ref[:, half:]
        left = dot(lhs[:, :half], a) - dot(lhs[:, half:], nb)
        right = dot(lhs[:, :half], nb) + dot(lhs[:, half:], a)
        return left.astype(BF16), right.astype(BF16)

    nt = lambda v: lax.dot_general(v, onehot, (((1,), (1,)), ((), ())), preferred_element_type=F32)
    left, right = times(across, w_ref)
    coupled = jnp.concatenate([nt(left), nt(right)], axis=1).astype(BF16)
    left, right = times(coupled, q_ref)
    through = jnp.concatenate([dot(left, onehot), dot(right, onehot)], axis=1)
    sign = row_sign(flags_ref, rows)
    coupled_ref[...] = (coupled.astype(F32) * sign).astype(BF16)
    through_ref[...] = (through * sign).astype(BF16)


def product_kernel(pieces, n_in, has_direct, flags_ref, lhs_ref, *rest):
    refs = rest[:n_in]
    rest = rest[n_in:]
    if has_direct:
        direct_ref, rest = rest[0], rest[1:]
    out_ref, even_ref, odd_ref, swap_ref, sign_ref = rest[-5:]
    half = even_ref.shape[0]
    wide = swap_ref.shape[0]

    @pl.when(pl.program_id(0) == 0)
    def _():
        r, c = iota((wide, wide), 0), iota((wide, wide), 1)
        plus = (c == r + 1) & (r % 2 == 0)
        minus = (r == c + 1) & (c % 2 == 0)
        swap_ref[...] = (plus.astype(F32) - minus.astype(F32)).astype(BF16)
        if has_direct:
            sign_ref[...] = jnp.broadcast_to(row_sign(flags_ref, sign_ref.shape[0]), sign_ref.shape)

    place(pieces, refs, even_ref, slice(None))
    for g in range(even_ref.shape[1] // wide):
        cols = slice(g * wide, (g + 1) * wide)
        odd_ref[:, cols] = dot(even_ref[:, cols], swap_ref[...]).astype(BF16)
    out = dot(lhs_ref[:, :half], even_ref[...]) + dot(lhs_ref[:, half:], odd_ref[...])
    if has_direct:
        out += direct_ref[...].astype(F32) * sign_ref[:, :1]
    out_ref[...] = out.astype(BF16)


def product(out, flags, lhs, arrays, pieces, width, skip, ext, at_in, at_out, n_out):
    rows, idim = lhs.shape
    full = lambda a: pl.BlockSpec(a.shape, lambda j: (0, 0))
    in_specs = [pl.BlockSpec(memory_space=pltpu.SMEM), full(lhs)]
    in_specs += [
        pl.BlockSpec((a.shape[0], TILE), functools.partial(lambda s, j: (0, j + s), s))
        for a, s in zip(arrays, skip)
    ]
    args = [flags, lhs, *arrays]
    if ext is not None:
        in_specs.append(pl.BlockSpec((rows, TILE), lambda j: (0, j + at_in)))
        args.append(ext)
    alias = {}
    if out is not None:
        alias = {len(args): 0}
        in_specs.append(pl.BlockSpec(memory_space=pl.ANY))
        args.append(out)
    return pl.pallas_call(
        functools.partial(product_kernel, pieces, len(arrays), ext is not None),
        grid=(width // TILE,),
        in_specs=in_specs,
        out_specs=pl.BlockSpec((rows, TILE), lambda j: (0, j + at_out)),
        out_shape=jax.ShapeDtypeStruct((rows, n_out), BF16),
        scratch_shapes=[
            pltpu.VMEM((idim // 2, TILE), BF16),
            pltpu.VMEM((idim // 2, TILE), BF16),
            pltpu.VMEM((256, 256), BF16),
            pltpu.VMEM((rows, 128), F32),
        ],
        input_output_aliases=alias,
        cost_estimate=pl.CostEstimate(
            flops=2 * rows * idim * width, transcendentals=0, bytes_accessed=4 * rows * width
        ),
    )(*args)


def code(x, y, z, c):
    return (((x % 4) * 2 + y % 2) * 2 + c) * 8 + (z % 4) * 2 + (y % 4) // 2


def route(move):
    pairs = []
    for x in range(4):
        for y in range(4):
            for z in range(4):
                for c in range(2):
                    pairs.append((code(x, y, z, c), code(*move(x, y, z), c)))
    return pairs


ROUTES = {
    "x": route(lambda x, y, z: (x ^ 1, y, z)),
    "y": route(lambda x, y, z: (x, y + 2, z)),
    "xy": route(lambda x, y, z: (x ^ 1, y + 2, z)),
    "z+": route(lambda x, y, z: (x, y, z + 1)),
    "z-": route(lambda x, y, z: (x, y, z - 1)),
    "z2": route(lambda x, y, z: (x, y, z + 2)),
}


def send(array, name):
    return lax.ppermute(array, ("leaf", "panel"), ROUTES[name])


def per_device(ext_rows, iface_rows, inverse, pivot, flags):
    ext = ext_rows[0]
    iface = iface_rows[0]
    winv = inverse[0]
    rows = ext.shape[0]
    idim = winv.shape[1]
    edim = ext.shape[1] - idim
    half = iface.shape[0] // 2
    c0 = 5 * TILE
    c1 = edim - c0
    first, own, far = pl.pallas_call(
        split_kernel,
        out_shape=(
            jax.ShapeDtypeStruct((half, c0), BF16),
            jax.ShapeDtypeStruct((half, idim + c1), BF16),
            jax.ShapeDtypeStruct((half, idim + c1), BF16),
        ),
    )(iface, winv)
    far_x = send(far, "x")
    own_y = send(own, "y")
    far_xy = send(far, "xy")
    first_z = [send(first, "z+"), send(first, "z-"), send(first, "z2")]
    mine = jnp.concatenate([own, own_y], axis=0)
    mine_z = [send(mine, d) for d in ("z+", "z-", "z2")]
    theirs = jnp.concatenate([far_x, far_xy], axis=0)
    theirs_z = [send(theirs, d) for d in ("z+", "z-", "z2")]
    ring = jnp.concatenate([first, *first_z], axis=0)
    ring_x = send(ring, "x")
    ring_y = send(ring, "y")
    mid = c0 // 2
    ring_xy0 = send(ring_y[:, :mid], "x")
    ring_xy1 = send(ring_x[:, mid:], "y")
    ring_xy = jnp.concatenate([ring_xy0, ring_xy1], axis=1)

    turns = (0, -1, 1, 2)
    late = lambda start: [(start + i, half * dy, dz, dy) for i, dz in enumerate(turns) for dy in (0, 1)]
    early = [(dy, half * i, dz, dy) for i, dz in enumerate(turns) for dy in (0, 1)]
    full = lambda a: pl.BlockSpec(a.shape, lambda j: (0, 0))
    narrow = lambda a: pl.BlockSpec((a.shape[0], idim), lambda j: (0, 0))
    blocks = [mine, *mine_z, theirs, *theirs_z]
    coupled, through = pl.pallas_call(
        functools.partial(couple_kernel, late(0), late(4), len(blocks)),
        grid=(1,),
        out_specs=(pl.BlockSpec((rows, idim), lambda j: (0, 0)),) * 2,
        in_specs=[
            pl.BlockSpec((rows, idim), lambda j: (0, edim // idim)),
            full(pivot),
            pl.BlockSpec(memory_space=pltpu.SMEM),
            *[narrow(a) for a in blocks],
        ],
        out_shape=(
            jax.ShapeDtypeStruct((rows, idim), BF16),
            jax.ShapeDtypeStruct((rows, idim), BF16),
        ),
        scratch_shapes=[pltpu.VMEM((idim // 2, idim), BF16)] * 2,
    )(ext, pivot, flags, *blocks)

    t0 = c0 // TILE
    te = edim // TILE
    skip = idim // TILE
    run = functools.partial(product, n_out=2 * edim)
    out = run(None, flags, through, [mine, *mine_z], late(0), c1, [skip] * 4, ext, t0, t0)
    out = run(out, flags, through, [ring, ring_y], early, c0, [0, 0], ext, 0, 0)
    out = run(out, flags, coupled, [ring_x, ring_xy], early, c0, [0, 0], None, 0, te)
    out = run(out, flags, coupled, [theirs, *theirs_z], late(0), c1, [skip] * 4, None, 0, te + t0)
    return out[None]


def solution(mesh):
    placed = (
        P("leaf", "panel", None),
        P("leaf", "panel", None),
        P("leaf", "panel", None),
        P("leaf", None),
        P("leaf", None),
    )
    return jax.shard_map(
        per_device, mesh=mesh, in_specs=placed, out_specs=P("leaf", "panel", None), check_vma=False
    )
```

```python
import functools

import jax
import jax.numpy as jnp
from jax import lax
from jax.experimental import pallas as pl
from jax.experimental.pallas import tpu as pltpu
from jax.sharding import PartitionSpec as P


FPTS = 256
BIT = 2
TILE = 768
SHIFTS = ((0, 0), (0, 1), (-1, 0), (-1, 1), (1, 0), (1, 1), (2, 0), (2, 1))
F32 = jnp.float32
BF16 = jnp.bfloat16


def iota(shape, axis):
    return lax.broadcasted_iota(jnp.int32, shape, axis)


def dot(a, b):
    return jnp.dot(a, b, preferred_element_type=F32)


def row_sign(flags_ref, rows):
    first = lax.axis_index("panel") * rows
    face = (first + iota((rows, 1), 0)) // (2 * FPTS)
    sign = jnp.ones((rows, 1), F32)
    for f in range(flags_ref.shape[1]):
        sign = jnp.where((face == f) & (flags_ref[0, f] == 1), -1.0, sign)
    return sign


def block_index(where, block):
    panel = lax.axis_index("panel")
    z, y = panel // 2, panel % 2
    out = jnp.zeros_like(where)
    for i, (dz, dy) in enumerate(SHIFTS):
        start = (((z + 4 + dz) % 4) * 2 + (y + dy) % 2) * block
        out = jnp.where(where // block == i, start + where % block, out)
    return out


def split_kernel(iface_ref, winv_ref, far_ref, own_ref, inward_ref):
    rows = iface_ref.shape[0]
    half = rows // 2
    idim = winv_ref.shape[1]
    edim = iface_ref.shape[1] - idim
    pick = (iota((half, rows), 1) == 2 * iota((half, rows), 0)).astype(BF16)
    even = dot(pick, iface_ref[...]).astype(BF16)
    winv = dot(pick, winv_ref[...]).astype(BF16)
    col = iota((1, idim), 1)
    src = jnp.where(col < idim // 2, 2 * col, 2 * col - idim + 1)
    deint = (iota((idim, idim), 0) == src).astype(BF16)
    far_ref[...] = even[:, :edim]
    own_ref[:, :edim] = even[:, :edim]
    own_ref[:, edim : edim + idim] = dot(winv, deint).astype(BF16)
    inward_ref[...] = dot(even[:, edim:], deint).astype(BF16)


def couple_kernel(edim, ext_ref, pivot_ref, flags_ref, *rest):
    blocks = rest[:8]
    coupled_ref, through_ref = rest[8:]
    rows = ext_ref.shape[0]
    idim = ext_ref.shape[1] - edim
    half = idim // 2
    block = half // 8
    gather = lambda at: jnp.concatenate([b[:, at : at + idim] for b in blocks], axis=0)
    winv, inward = gather(edim), gather(edim + idim)
    col = iota((1, idim), 1)
    part = (col >= half).astype(jnp.int32)
    src = 2 * block_index(col - half * part, block) + part
    deint = (iota((idim, idim), 0) == src).astype(BF16)
    across = dot(ext_ref[:, edim:], deint).astype(BF16)
    pivot = pivot_ref[...]
    spread = (block_index(iota((half, 1), 0), block) == pivot).astype(BF16)
    chosen = (iota((half, half), 0) == block_index(iota((1, half), 1), block)).astype(BF16)
    back = dot((iota((half, half), 0) == pivot).astype(BF16), chosen).astype(BF16)

    def times(lhs, even):
        a, nb = even[:, :half], even[:, half:]
        left = dot(lhs[:, :half], a) - dot(lhs[:, half:], nb)
        right = dot(lhs[:, :half], nb) + dot(lhs[:, half:], a)
        return left.astype(BF16), right.astype(BF16)

    nt = lambda v: lax.dot_general(v, spread, (((1,), (1,)), ((), ())), preferred_element_type=F32)
    left, right = times(across, winv)
    coupled = jnp.concatenate([nt(left), nt(right)], axis=1)
    left, right = times(coupled.astype(BF16), inward)
    through = jnp.concatenate([dot(left, back), dot(right, back)], axis=1)
    sign = row_sign(flags_ref, rows)
    coupled_ref[...] = (coupled * sign).astype(BF16)
    through_ref[...] = (through * sign).astype(BF16)


def product_kernel(edim, at, own, *refs):
    if own:
        flags_ref, ext_ref, lhs_ref, *refs = refs
    else:
        lhs_ref, *refs = refs
    blocks, refs = refs[:8], refs[8:]
    if not own:
        refs = refs[1:]
    out_ref, held, sems = refs
    rows, idim = lhs_ref.shape
    half = idim // 2
    wide = 256
    r, c = iota((wide, wide), 0), iota((wide, wide), 1)
    plus = (c == r + 1) & (r % 2 == 0)
    minus = (r == c + 1) & (c % 2 == 0)
    swap = (plus.astype(F32) - minus.astype(F32)).astype(BF16)
    sign = row_sign(flags_ref, rows) if own else None
    copies = []
    for t in range(edim // TILE):
        for g in range(t * TILE, (t + 1) * TILE, wide):
            cols = slice(g, g + wide)
            even = jnp.concatenate([b[:, cols] for b in blocks], axis=0)
            odd = dot(even, swap).astype(BF16)
            out = dot(lhs_ref[...], jnp.concatenate([even, odd], axis=0))
            if own:
                out += ext_ref[:, cols].astype(F32) * sign
            held[:, cols] = out.astype(BF16)
        cols = pl.ds(t * TILE, TILE)
        copy = pltpu.make_async_copy(
            held.at[:, cols], out_ref.at[:, pl.ds(at + t * TILE, TILE)], sems.at[t]
        )
        copy.start()
        copies.append(copy)
    for copy in copies:
        copy.wait()


VMEM = pl.BlockSpec(memory_space=pltpu.VMEM)
SMEM = pl.BlockSpec(memory_space=pltpu.SMEM)
ANY = pl.BlockSpec(memory_space=pl.ANY)


def product(lhs, blocks, edim, ext=None, flags=None, out=None):
    rows, idim = lhs.shape
    own = out is None
    if own:
        args = [flags, ext, lhs, *blocks]
        specs = [SMEM] + [VMEM] * (len(args) - 1)
        alias = {}
    else:
        args = [lhs, *blocks, out]
        specs = [VMEM] * (len(args) - 1) + [ANY]
        alias = {len(args) - 1: 0}
    return pl.pallas_call(
        functools.partial(product_kernel, edim, 0 if own else edim, own),
        in_specs=specs,
        out_specs=ANY,
        out_shape=jax.ShapeDtypeStruct((rows, 2 * edim), BF16),
        scratch_shapes=[
            pltpu.VMEM((rows, edim), BF16),
            pltpu.SemaphoreType.DMA((edim // TILE,)),
        ],
        input_output_aliases=alias,
        cost_estimate=pl.CostEstimate(
            flops=2 * rows * idim * edim, transcendentals=0, bytes_accessed=4 * rows * edim
        ),
    )(*args)


def code(x, y, z, c):
    return (((x % 4) * 2 + y % 2) * 2 + c) * 8 + (z % 4) * 2 + (y % 4) // 2


def route(move):
    pairs = []
    for x in range(4):
        for y in range(4):
            for z in range(4):
                for c in range(2):
                    pairs.append((code(x, y, z, c), code(*move(x, y, z), c)))
    return pairs


ROUTES = {
    "x": route(lambda x, y, z: (x ^ 1, y, z)),
    "y": route(lambda x, y, z: (x, y + 2, z)),
    "xy": route(lambda x, y, z: (x ^ 1, y + 2, z)),
    "z+": route(lambda x, y, z: (x, y, z + 1)),
    "z-": route(lambda x, y, z: (x, y, z - 1)),
    "z2": route(lambda x, y, z: (x, y, z + 2)),
}


def send(array, name):
    return lax.ppermute(array, ("leaf", "panel"), ROUTES[name])


def per_device(ext_rows, iface_rows, inverse, pivot, flags):
    ext = ext_rows[0]
    iface = iface_rows[0]
    winv = inverse[0]
    rows = ext.shape[0]
    idim = winv.shape[1]
    edim = ext.shape[1] - idim
    half = iface.shape[0] // 2
    shape = lambda r, c: jax.ShapeDtypeStruct((r, c), BF16)
    far, own, inward = pl.pallas_call(
        split_kernel,
        in_specs=[VMEM] * 2,
        out_specs=(VMEM,) * 3,
        out_shape=(shape(half, edim), shape(half, edim + 2 * idim), shape(half, idim)),
    )(iface, winv)
    own = lax.dynamic_update_slice(own, send(inward, "x"), (0, edim + idim))
    x = send(far, "x")
    z2 = send(own, "z2")
    y = send(own, "y")
    zp = send(own, "z+")
    zm = send(own, "z-")
    x_zp = send(x, "z+")
    x_zm = send(x, "z-")
    y_zp = send(y, "z+")
    y_zm = send(y, "z-")
    xy = send(y, "x")
    x_z2 = send(z2, "x")
    y_z2 = send(z2, "y")
    xy_zp = send(y_zp, "x")
    xy_zm = send(x_zm, "y")
    xy_z2 = send(x_z2, "y")
    mine = [own, y, zp, y_zp, zm, y_zm, z2, y_z2]
    theirs = [x, xy, x_zp, xy_zp, x_zm, xy_zm, x_z2, xy_z2]
    coupled, through = pl.pallas_call(
        functools.partial(couple_kernel, edim),
        in_specs=[VMEM, VMEM, SMEM] + [VMEM] * 8,
        out_specs=(VMEM,) * 2,
        out_shape=(shape(rows, idim),) * 2,
    )(ext, pivot, flags, *mine)
    out = product(through, mine, edim, ext=ext, flags=flags)
    out = product(coupled, theirs, edim, out=out)
    return out[None]


def solution(mesh):
    placed = (
        P("leaf", "panel", None),
        P("leaf", "panel", None),
        P("leaf", "panel", None),
        P("leaf", None),
        P("leaf", None),
    )
    return jax.shard_map(
        per_device, mesh=mesh, in_specs=placed, out_specs=P("leaf", "panel", None), check_vma=False
    )
```

```python
import functools

import jax
import jax.numpy as jnp
from jax import lax
from jax.experimental import pallas as pl
from jax.experimental.pallas import tpu as pltpu
from jax.sharding import PartitionSpec as P


FPTS = 256
TILE = 768
VMEM_LIMIT = 28 * 2**20
SHIFTS = ((0, 0), (0, 1), (-1, 0), (-1, 1), (1, 0), (1, 1), (2, 0), (2, 1))
F32 = jnp.float32
BF16 = jnp.bfloat16


def kernel_call(body, **kwargs):
    return pl.pallas_call(
        body, compiler_params=pltpu.CompilerParams(vmem_limit_bytes=VMEM_LIMIT), **kwargs
    )


def iota(shape, axis):
    return lax.broadcasted_iota(jnp.int32, shape, axis)


def dot(a, b):
    return jnp.dot(a, b, preferred_element_type=F32)


def row_sign(flags_ref, rows):
    first = lax.axis_index("panel") * rows
    face = (first + iota((rows, 1), 0)) // (2 * FPTS)
    sign = jnp.ones((rows, 1), F32)
    for f in range(flags_ref.shape[1]):
        sign = jnp.where((face == f) & (flags_ref[0, f] == 1), -1.0, sign)
    return sign


def block_index(where, block):
    panel = lax.axis_index("panel")
    z, y = panel // 2, panel % 2
    out = jnp.zeros_like(where)
    for i, (dz, dy) in enumerate(SHIFTS):
        start = (((z + 4 + dz) % 4) * 2 + (y + dy) % 2) * block
        out = jnp.where(where // block == i, start + where % block, out)
    return out


def even_rows(rows):
    return (iota((rows // 2, rows), 1) == 2 * iota((rows // 2, rows), 0)).astype(BF16)


def split_columns(size):
    col = iota((1, size), 1)
    src = jnp.where(col < size // 2, 2 * col, 2 * col - size + 1)
    return (iota((size, size), 0) == src).astype(BF16)


def inward_kernel(iface_ref, inward_ref, held, sem):
    idim = held.shape[1]
    edim = iface_ref.shape[1] - idim
    copy = pltpu.make_async_copy(iface_ref.at[:, pl.ds(edim, idim)], held, sem)
    copy.start()
    deint = split_columns(idim)
    copy.wait()
    inward_ref[...] = dot(dot(even_rows(held.shape[0]), held[...]).astype(BF16), deint).astype(BF16)


def split_kernel(iface_ref, winv_ref, far_ref, own_ref):
    pick = even_rows(iface_ref.shape[0])
    edim = far_ref.shape[1]
    idim = winv_ref.shape[1]
    even = dot(pick, iface_ref[:, :edim]).astype(BF16)
    far_ref[...] = even
    own_ref[:, :edim] = even
    winv = dot(pick, winv_ref[...]).astype(BF16)
    own_ref[:, edim : edim + idim] = dot(winv, split_columns(idim)).astype(BF16)


def prep_kernel(edim, ext_ref, pivot_ref, across_ref, spread_ref, back_ref):
    idim = ext_ref.shape[1] - edim
    half = idim // 2
    block = half // 8
    col = iota((1, idim), 1)
    part = (col >= half).astype(jnp.int32)
    src = 2 * block_index(col - half * part, block) + part
    deint = (iota((idim, idim), 0) == src).astype(BF16)
    pivot = pivot_ref[...]
    spread_ref[...] = (block_index(iota((half, 1), 0), block) == pivot).astype(BF16)
    chosen = (iota((half, half), 0) == block_index(iota((1, half), 1), block)).astype(BF16)
    back_ref[...] = dot((iota((half, half), 0) == pivot).astype(BF16), chosen).astype(BF16)
    across_ref[...] = dot(ext_ref[:, edim:], deint).astype(BF16)


def couple_kernel(edim, flags_ref, across_ref, spread_ref, back_ref, *rest):
    blocks = rest[:8]
    coupled_ref, through_ref = rest[8:]
    rows, idim = across_ref.shape
    half = idim // 2
    gather = lambda at: jnp.concatenate([b[:, at : at + idim] for b in blocks], axis=0)
    spread, back = spread_ref[...], back_ref[...]
    sign = row_sign(flags_ref, rows)

    def times(lhs, even):
        a, nb = even[:, :half], even[:, half:]
        left = dot(lhs[:, :half], a) - dot(lhs[:, half:], nb)
        right = dot(lhs[:, :half], nb) + dot(lhs[:, half:], a)
        return left.astype(BF16), right.astype(BF16)

    nt = lambda v: lax.dot_general(v, spread, (((1,), (1,)), ((), ())), preferred_element_type=F32)
    left, right = times(across_ref[...], gather(edim))
    coupled = jnp.concatenate([nt(left), nt(right)], axis=1)
    left, right = times(coupled.astype(BF16), gather(edim + idim))
    through = jnp.concatenate([dot(left, back), dot(right, back)], axis=1)
    coupled_ref[...] = (coupled * sign).astype(BF16)
    through_ref[...] = (through * sign).astype(BF16)


def product_kernel(edim, at, own, *refs):
    if own:
        flags_ref, lhs_ref, ext_ref, *refs = refs
    else:
        lhs_ref, *refs = refs
    blocks, refs = refs[:8], refs[8:]
    out_ref, held, out_sems = refs[-3:]
    rows, idim = lhs_ref.shape
    wide = 256
    tiles = edim // TILE
    sign = row_sign(flags_ref, rows) if own else None
    is_even = iota((idim // 2, wide), 1) % 2 == 0
    stores = []
    for t in range(tiles):
        for g in range(t * TILE, (t + 1) * TILE, wide):
            cols = slice(g, g + wide)
            even = jnp.concatenate([b[:, cols] for b in blocks], axis=0)
            wider = even.astype(F32)
            odd = jnp.where(is_even, -pltpu.roll(wider, wide - 1, 1), pltpu.roll(wider, 1, 1))
            out = dot(lhs_ref[...], jnp.concatenate([even, odd.astype(BF16)], axis=0))
            if own:
                out += ext_ref[:, cols].astype(F32) * sign
            held[:, cols] = out.astype(BF16)
        store = pltpu.make_async_copy(
            held.at[:, pl.ds(t * TILE, TILE)],
            out_ref.at[:, pl.ds(at + t * TILE, TILE)],
            out_sems.at[t],
        )
        store.start()
        stores.append(store)
    for store in stores:
        store.wait()


def near(array):
    return pltpu.with_memory_space_constraint(array, pltpu.VMEM)


VMEM = pl.BlockSpec(memory_space=pltpu.VMEM)
SMEM = pl.BlockSpec(memory_space=pltpu.SMEM)
ANY = pl.BlockSpec(memory_space=pl.ANY)


def product(lhs, blocks, edim, ext=None, flags=None, out=None):
    rows, idim = lhs.shape
    own = out is None
    tiles = edim // TILE
    if own:
        args = [flags, near(lhs), near(ext), *map(near, blocks)]
        specs = [SMEM] + [VMEM] * 10
        alias = {}
    else:
        args = [near(lhs), *map(near, blocks), out]
        specs = [VMEM] * 9 + [ANY]
        alias = {len(args) - 1: 0}
    scratch = [
        pltpu.VMEM((rows, edim), BF16),
        pltpu.SemaphoreType.DMA((tiles,)),
    ]
    return kernel_call(
        functools.partial(product_kernel, edim, 0 if own else edim, own),
        in_specs=specs,
        out_specs=ANY,
        out_shape=jax.ShapeDtypeStruct((rows, 2 * edim), BF16),
        scratch_shapes=scratch,
        input_output_aliases=alias,
        cost_estimate=pl.CostEstimate(
            flops=2 * rows * idim * edim, transcendentals=0, bytes_accessed=4 * rows * edim
        ),
    )(*args)


def code(x, y, z, c):
    return (((x % 4) * 2 + y % 2) * 2 + c) * 8 + (z % 4) * 2 + (y % 4) // 2


def route(move):
    pairs = []
    for x in range(4):
        for y in range(4):
            for z in range(4):
                for c in range(2):
                    pairs.append((code(x, y, z, c), code(*move(x, y, z), c)))
    return pairs


ROUTES = {
    "x": route(lambda x, y, z: (x ^ 1, y, z)),
    "y": route(lambda x, y, z: (x, y + 2, z)),
    "xy": route(lambda x, y, z: (x ^ 1, y + 2, z)),
    "z+": route(lambda x, y, z: (x, y, z + 1)),
    "z-": route(lambda x, y, z: (x, y, z - 1)),
    "z2": route(lambda x, y, z: (x, y, z + 2)),
}


def send(array, name):
    return lax.ppermute(array, ("leaf", "panel"), ROUTES[name])


def per_device(ext_rows, iface_rows, inverse, pivot, flags):
    return merge(ext_rows[0], iface_rows[0], inverse[0], pivot, flags)[None]


def merge(ext, iface, winv, pivot, flags):
    rows = ext.shape[0]
    idim = winv.shape[1]
    edim = ext.shape[1] - idim
    half = iface.shape[0] // 2
    shape = lambda r, c: jax.ShapeDtypeStruct((r, c), BF16)
    local = lambda r, c: pltpu.VMEM((r, c), BF16)
    inward = kernel_call(
        inward_kernel,
        in_specs=[ANY],
        out_specs=VMEM,
        out_shape=shape(half, idim),
        scratch_shapes=[pltpu.VMEM((2 * half, idim), BF16), pltpu.SemaphoreType.DMA(())],
    )(iface)
    inward = send(inward, "x")
    far, own = kernel_call(
        split_kernel,
        in_specs=[VMEM] * 2,
        out_specs=(VMEM,) * 2,
        out_shape=(local(half, edim), local(half, edim + 2 * idim)),
    )(iface, winv)
    own = lax.dynamic_update_slice(own, inward, (0, edim + idim))
    z2 = send(own, "z2")
    y = send(own, "y")
    x = send(far, "x")
    x_z2 = send(z2, "x")
    y_z2 = send(z2, "y")
    y_zp = send(y, "z+")
    y_zm = send(y, "z-")
    zp = send(own, "z+")
    zm = send(own, "z-")
    xy = send(x, "y")
    x_zp = send(x, "z+")
    x_zm = send(x, "z-")
    xy_zp = send(y_zp, "x")
    xy_z2 = send(x_z2, "y")
    xy_zm = send(y_zm, "x")
    mine = [own, y, zp, y_zp, zm, y_zm, z2, y_z2]
    theirs = [x, xy, x_zp, xy_zp, x_zm, xy_zm, x_z2, xy_z2]
    prep = kernel_call(
        functools.partial(prep_kernel, edim),
        in_specs=[VMEM, VMEM],
        out_specs=(VMEM,) * 3,
        out_shape=(local(rows, idim), local(idim // 2, idim // 2), local(idim // 2, idim // 2)),
    )(near(ext), pivot)
    coupled, through = kernel_call(
        functools.partial(couple_kernel, edim),
        in_specs=[SMEM] + [VMEM] * 11,
        out_specs=(VMEM,) * 2,
        out_shape=(local(rows, idim),) * 2,
    )(flags, *map(near, prep), *map(near, mine))
    out = product(through, mine, edim, ext=ext, flags=flags)
    return product(coupled, theirs, edim, out=out)


def solution(mesh):
    placed = (
        P("leaf", "panel", None),
        P("leaf", "panel", None),
        P("leaf", "panel", None),
        P("leaf", None),
        P("leaf", None),
    )
    return jax.shard_map(
        per_device, mesh=mesh, in_specs=placed, out_specs=P("leaf", "panel", None), check_vma=False
    )
```

```python
import functools

import jax
import jax.numpy as jnp
from jax import lax
from jax.experimental import pallas as pl
from jax.experimental.pallas import tpu as pltpu
from jax.sharding import PartitionSpec as P


FPTS = 256
TILE = 512
VMEM_LIMIT = 28 * 2**20
SHIFTS = ((0, 0), (0, 1), (-1, 0), (-1, 1), (1, 0), (1, 1), (2, 0), (2, 1))
F32 = jnp.float32
BF16 = jnp.bfloat16


def kernel_call(body, **kwargs):
    params = pltpu.CompilerParams(vmem_limit_bytes=VMEM_LIMIT)
    return pl.pallas_call(body, compiler_params=params, **kwargs)


def iota(shape, axis):
    return lax.broadcasted_iota(jnp.int32, shape, axis)


def dot(a, b):
    return jnp.dot(a, b, preferred_element_type=F32)


def row_sign(flags_ref, rows):
    first = lax.axis_index("panel") * rows
    face = (first + iota((rows, 1), 0)) // (2 * FPTS)
    sign = jnp.ones((rows, 1), F32)
    for f in range(flags_ref.shape[1]):
        sign = jnp.where((face == f) & (flags_ref[0, f] == 1), -1.0, sign)
    return sign


def block_index(where, block):
    panel = lax.axis_index("panel")
    z, y = panel // 2, panel % 2
    out = jnp.zeros_like(where)
    for i, (dz, dy) in enumerate(SHIFTS):
        start = (((z + 4 + dz) % 4) * 2 + (y + dy) % 2) * block
        out = jnp.where(where // block == i, start + where % block, out)
    return out


def even_rows(rows):
    return (iota((rows // 2, rows), 1) == 2 * iota((rows // 2, rows), 0)).astype(BF16)


def split_columns(size):
    col = iota((1, size), 1)
    src = jnp.where(col < size // 2, 2 * col, 2 * col - size + 1)
    return (iota((size, size), 0) == src).astype(BF16)


def inward_kernel(iface_ref, inward_ref, held, sem):
    idim = held.shape[1]
    edim = iface_ref.shape[1] - idim
    copy = pltpu.make_async_copy(iface_ref.at[:, pl.ds(edim, idim)], held, sem)
    copy.start()
    deint = split_columns(idim)
    copy.wait()
    inward_ref[...] = dot(dot(even_rows(held.shape[0]), held[...]).astype(BF16), deint).astype(BF16)


def split_kernel(iface_hbm, winv_hbm, far_ref, own_ref, iface_ref, winv_ref, sems):
    edim = far_ref.shape[1]
    idim = winv_ref.shape[1]
    wide = pltpu.make_async_copy(iface_hbm.at[:, pl.ds(0, edim)], iface_ref, sems.at[0])
    wide.start()
    square = pltpu.make_async_copy(winv_hbm, winv_ref, sems.at[1])
    square.start()
    pick = even_rows(iface_ref.shape[0])
    wide.wait()
    even = dot(pick, iface_ref[...]).astype(BF16)
    far_ref[...] = even
    own_ref[:, :edim] = even
    square.wait()
    winv = dot(pick, winv_ref[...]).astype(BF16)
    own_ref[:, edim : edim + idim] = dot(winv, split_columns(idim)).astype(BF16)


def prep_kernel(edim, flags_hbm, ext_hbm, pivot_hbm, *refs):
    across_ref, spread_ref, back_ref, sign_ref, held, pivot_ref, flags_ref, sems = refs
    idim = held.shape[1]
    loads = [
        pltpu.make_async_copy(pivot_hbm, pivot_ref, sems.at[0]),
        pltpu.make_async_copy(flags_hbm, flags_ref, sems.at[1]),
        pltpu.make_async_copy(ext_hbm.at[:, pl.ds(edim, idim)], held, sems.at[2]),
    ]
    for load in loads:
        load.start()
    half = idim // 2
    block = half // 8
    col = iota((1, idim), 1)
    part = (col >= half).astype(jnp.int32)
    src = 2 * block_index(col - half * part, block) + part
    deint = (iota((idim, idim), 0) == src).astype(BF16)
    loads[0].wait()
    pivot = pivot_ref[...]
    spread_ref[...] = (block_index(iota((half, 1), 0), block) == pivot).astype(BF16)
    chosen = (iota((half, half), 0) == block_index(iota((1, half), 1), block)).astype(BF16)
    back_ref[...] = dot((iota((half, half), 0) == pivot).astype(BF16), chosen).astype(BF16)
    loads[1].wait()
    sign_ref[...] = jnp.broadcast_to(row_sign(flags_ref, sign_ref.shape[0]), sign_ref.shape)
    loads[2].wait()
    across_ref[...] = dot(held[...], deint).astype(BF16)


def couple_kernel(edim, across_ref, spread_ref, back_ref, sign_ref, *rest):
    blocks = rest[:8]
    coupled_ref, through_ref = rest[8:]
    _, idim = across_ref.shape
    half = idim // 2
    gather = lambda at: jnp.concatenate([b[:, at : at + idim] for b in blocks], axis=0)
    spread, back = spread_ref[...], back_ref[...]
    sign = sign_ref[:, :1]

    def times(lhs, even):
        a, nb = even[:, :half], even[:, half:]
        left = dot(lhs[:, :half], a) - dot(lhs[:, half:], nb)
        right = dot(lhs[:, :half], nb) + dot(lhs[:, half:], a)
        return left.astype(BF16), right.astype(BF16)

    nt = lambda v: lax.dot_general(v, spread, (((1,), (1,)), ((), ())), preferred_element_type=F32)
    left, right = times(across_ref[...], gather(edim))
    coupled = jnp.concatenate([nt(left), nt(right)], axis=1)
    left, right = times(coupled.astype(BF16), gather(edim + idim))
    through = jnp.concatenate([dot(left, back), dot(right, back)], axis=1)
    coupled_ref[...] = (coupled * sign).astype(BF16)
    through_ref[...] = (through * sign).astype(BF16)


def product_kernel(edim, at, own, *refs):
    if own:
        sign_ref, lhs_ref, ext_ref, *refs = refs
    else:
        lhs_ref, *refs = refs
    blocks, refs = refs[:8], refs[8:]
    out_ref, held, out_sems = refs[-3:]
    _, idim = lhs_ref.shape
    wide = 256
    tiles = edim // TILE
    sign = sign_ref[:, :1] if own else None
    is_even = iota((idim // 2, wide), 1) % 2 == 0
    stores = []
    for t in range(tiles):
        for g in range(t * TILE, (t + 1) * TILE, wide):
            cols = slice(g, g + wide)
            even = jnp.concatenate([b[:, cols] for b in blocks], axis=0)
            wider = even.astype(F32)
            odd = jnp.where(is_even, -pltpu.roll(wider, wide - 1, 1), pltpu.roll(wider, 1, 1))
            out = dot(lhs_ref[...], jnp.concatenate([even, odd.astype(BF16)], axis=0))
            if own:
                out += ext_ref[:, cols].astype(F32) * sign
            held[:, cols] = out.astype(BF16)
        store = pltpu.make_async_copy(
            held.at[:, pl.ds(t * TILE, TILE)],
            out_ref.at[:, pl.ds(at + t * TILE, TILE)],
            out_sems.at[t],
        )
        store.start()
        stores.append(store)
    for store in stores:
        store.wait()


def distant(array):
    return pltpu.with_memory_space_constraint(array, pltpu.HBM)


def near(array):
    return pltpu.with_memory_space_constraint(array, pltpu.VMEM)


VMEM = pl.BlockSpec(memory_space=pltpu.VMEM)
SMEM = pl.BlockSpec(memory_space=pltpu.SMEM)
ANY = pl.BlockSpec(memory_space=pl.ANY)
HBM = pl.BlockSpec(memory_space=pltpu.HBM)


def product(lhs, blocks, edim, ext=None, sign=None, out=None):
    rows, idim = lhs.shape
    own = out is None
    tiles = edim // TILE
    if own:
        args = [near(sign), near(lhs), near(ext), *map(near, blocks)]
        specs = [VMEM] * 11
        alias = {}
    else:
        args = [near(lhs), *map(near, blocks), out]
        specs = [VMEM] * 9 + [ANY]
        alias = {len(args) - 1: 0}
    scratch = [
        pltpu.VMEM((rows, edim), BF16),
        pltpu.SemaphoreType.DMA((tiles,)),
    ]
    return kernel_call(
        functools.partial(product_kernel, edim, 0 if own else edim, own),
        in_specs=specs,
        out_specs=ANY,
        out_shape=jax.ShapeDtypeStruct((rows, 2 * edim), BF16),
        scratch_shapes=scratch,
        input_output_aliases=alias,
        cost_estimate=pl.CostEstimate(
            flops=2 * rows * idim * edim, transcendentals=0, bytes_accessed=4 * rows * edim
        ),
    )(*args)


def code(x, y, z, c):
    return (((x % 4) * 2 + y % 2) * 2 + c) * 8 + (z % 4) * 2 + (y % 4) // 2


def route(move):
    pairs = []
    for x in range(4):
        for y in range(4):
            for z in range(4):
                for c in range(2):
                    pairs.append((code(x, y, z, c), code(*move(x, y, z), c)))
    return pairs


ROUTES = {
    "x": route(lambda x, y, z: (x ^ 1, y, z)),
    "y": route(lambda x, y, z: (x, y + 2, z)),
    "xy": route(lambda x, y, z: (x ^ 1, y + 2, z)),
    "z+": route(lambda x, y, z: (x, y, z + 1)),
    "z-": route(lambda x, y, z: (x, y, z - 1)),
    "z2": route(lambda x, y, z: (x, y, z + 2)),
}


def send(array, name):
    return lax.ppermute(array, ("leaf", "panel"), ROUTES[name])


def per_device(ext_rows, iface_rows, inverse, pivot, flags):
    return merge(ext_rows[0], iface_rows[0], inverse[0], pivot, flags)[None]


def merge(ext, iface, winv, pivot, flags):
    rows = ext.shape[0]
    idim = winv.shape[1]
    edim = ext.shape[1] - idim
    half = iface.shape[0] // 2
    local = lambda r, c: pltpu.VMEM((r, c), BF16)
    inward = kernel_call(
        inward_kernel,
        in_specs=[HBM],
        out_specs=VMEM,
        out_shape=local(half, idim),
        scratch_shapes=[pltpu.VMEM((2 * half, idim), BF16), pltpu.SemaphoreType.DMA(())],
    )(distant(iface))
    inward = send(inward, "x")
    far, own = kernel_call(
        split_kernel,
        in_specs=[HBM] * 2,
        out_specs=(VMEM,) * 2,
        out_shape=(local(half, edim), local(half, edim + 2 * idim)),
        scratch_shapes=[
            pltpu.VMEM((2 * half, edim), BF16),
            pltpu.VMEM((2 * half, idim), BF16),
            pltpu.SemaphoreType.DMA((2,)),
        ],
    )(distant(iface), distant(winv))
    own = lax.dynamic_update_slice(own, inward, (0, edim + idim))
    z2 = send(own, "z2")
    y = send(own, "y")
    x = send(far, "x")
    zp = send(own, "z+")
    zm = send(own, "z-")
    xy = send(x, "y")
    x_z2 = send(z2[:, :edim], "x")
    y_zp = send(y, "z+")
    y_zm = send(y, "z-")
    y_z2 = send(z2, "y")
    x_zp = send(zp[:, :edim], "x")
    x_zm = send(zm[:, :edim], "x")
    xy_zp = send(xy, "z+")
    xy_zm = send(xy, "z-")
    xy_z2 = send(x_z2, "y")
    mine = [own, y, zp, y_zp, zm, y_zm, z2, y_z2]
    theirs = [x, xy, x_zp, xy_zp, x_zm, xy_zm, x_z2, xy_z2]
    prep = kernel_call(
        functools.partial(prep_kernel, edim),
        in_specs=[HBM] * 3,
        out_specs=(VMEM,) * 4,
        out_shape=(
            local(rows, idim),
            local(idim // 2, idim // 2),
            local(idim // 2, idim // 2),
            pltpu.VMEM((rows, 128), F32),
        ),
        scratch_shapes=[
            pltpu.VMEM((rows, idim), BF16),
            pltpu.VMEM(pivot.shape, jnp.int32),
            pltpu.SMEM(flags.shape, jnp.int32),
            pltpu.SemaphoreType.DMA((3,)),
        ],
    )(distant(flags), distant(ext), distant(pivot))
    coupled, through = kernel_call(
        functools.partial(couple_kernel, edim),
        in_specs=[VMEM] * 12,
        out_specs=(VMEM,) * 2,
        out_shape=(local(rows, idim),) * 2,
    )(*map(near, prep), *map(near, mine))
    out = product(through, mine, edim, ext=ext, sign=prep[-1])
    return product(coupled, theirs, edim, out=out)


def solution(mesh):
    placed = (
        P("leaf", "panel", None),
        P("leaf", "panel", None),
        P("leaf", "panel", None),
        P("leaf", None),
        P("leaf", None),
    )
    return jax.shard_map(
        per_device, mesh=mesh, in_specs=placed, out_specs=P("leaf", "panel", None), check_vma=False
    )
```
